256 devices in a mesh: group: 16 (over z_lo, y), fsdp: 16 (over x, z_hi, core).
Axes of the slice: x: 4, y: 4, z: 8 (z_hi: 2, z_lo: 4; z = z_hi * 4 + z_lo), core: 2. Of those that a mesh axis runs over, the one named last changes fastest.
Arguments:
- frames: bfloat16 [16, 8192, 1280], P('group', 'fsdp'), may hold values from -6 to 6
- cotangent: bfloat16 [16, 8192, 1280], P('group', 'fsdp'), may hold values from -12 to 12
- mix_partner: int32 [16, 64], P('group', 'fsdp'), may hold values from 0 to 3
- lengths: int32 [16, 64], P('group', 'fsdp'), may hold values from 32 to 128, as said below
- inner_params: bfloat16 [16, 1280, 2, 2560], P('group', 'fsdp'), may hold values from -6 to 6
- first_moment: float32 [16, 1280, 2, 2560], P('group', 'fsdp'), may hold values from -6 to 6
- second_moment: float32 [16, 1280, 2, 2560], P('group', 'fsdp'), may hold values from 0.25 to 4
- outer_params: float32 [1280, 2, 2560], P('fsdp'), may hold values from -6 to 6
- momentum: float32 [1280, 2, 2560], P('fsdp'), may hold values from -3 to 3
Outputs:
- new_moment: float32 [16, 1280, 2, 2560], P('group', 'fsdp')
- new_outer: float32 [1280, 2, 2560], P('fsdp')
- new_momentum: float32 [1280, 2, 2560], P('fsdp')
The draws below stay inside these ranges and needn't reach their ends.
Inputs may be any that keep to these rules, and one draw needn't show every extreme that they name: `lengths`: in every replica at least one utterance has all 128 frames.
All inputs are finite; a program needn't handle non-finite values.
Results may differ from the reference program's by a relative error of at most 0.004.
Values may be sent and summed in bfloat16 or wider, within the bound.
A program may use at most 128 MiB of HBM per device.

```python
import math
import jax
import jax.numpy as jnp
from jax import lax

D = 1280
FF = 2560
TOK_DEV = 512
FR = 128
UTT_DEV = 4
UTTS = 64
TOKENS = 8192
GROUPS = 16
N_FSDP = 16


def draw_lengths(key, part):
    first_key = jax.random.fold_in(key, 11)
    second_key = jax.random.fold_in(key, 23)
    drawn = jax.random.randint(first_key, (GROUPS, UTTS), FR // 4, FR + 1)
    chosen = jax.random.randint(second_key, (GROUPS, 1), 0, UTTS)
    slots = lax.broadcasted_iota(jnp.int32, (GROUPS, UTTS), 1)
    return jnp.where(slots == chosen, FR, drawn).astype(jnp.int32)


def set_ends(entries, rng, low, high):
    place = [jax.random.randint(jax.random.fold_in(rng, axis), (), 0, length) for axis, length in enumerate(entries.shape)]
    longest = entries.shape.index(max(entries.shape))
    beside = place[:longest] + [(place[longest] + 1) % entries.shape[longest]] + place[longest + 1:]
    return entries.at[tuple(place)].set(low).at[tuple(beside)].set(high)


def levels(stream_key, extent, split, smallest, largest):
    level, own = 1.0, jax.random.fold_in(stream_key, 6)
    for position, blocks in split:
        heights = jnp.exp(jax.random.uniform(jax.random.fold_in(own, position), (blocks,), jnp.float32, smallest / len(split), largest / len(split)))
        level = level * jnp.repeat(heights, extent[position] // blocks).reshape([-1 if axis == position else 1 for axis in range(len(extent))])
    return level


def noise(rng, shape, deviation, most, split=(), dtype=jnp.bfloat16):
    factor_of = levels(rng, shape, split, -0.22, 0.18) if split else 1.0
    array = jax.random.normal(rng, shape, jnp.float32) * deviation * factor_of
    return jnp.minimum(jnp.maximum(array, -most), most).astype(dtype)


def setup_inputs(seed: int = 0) -> dict:
    streams_of = jax.random.split(jax.random.key(seed), 10)
    frames = noise(streams_of[0], (GROUPS, TOKENS, D), 1.0, 6.0, ((0, 16), (1, 16)))
    cotangent = noise(streams_of[1], (GROUPS, TOKENS, D), 2.0, 12.0, ((0, 16), (1, 16)))
    mix_partner = set_ends(jax.random.randint(streams_of[2], (GROUPS, UTTS), 0, UTT_DEV), jax.random.fold_in(streams_of[2], 1), 0, UTT_DEV - 1).astype(jnp.int32)
    lengths = draw_lengths(jax.random.fold_in(streams_of[9], 71), 0)
    inner_params = noise(streams_of[4], (GROUPS, D, 2, FF), 1.0, 6.0, ((0, 16), (1, 16)))
    first_moment = noise(streams_of[5], (GROUPS, D, 2, FF), 1.0, 6.0, ((0, 16), (1, 16)), jnp.float32)
    second_moment = jnp.clip(jnp.exp(math.log(4.0) - 2.7725887 * jax.random.uniform(streams_of[6], (GROUPS, D, 2, FF), jnp.float32) ** levels(streams_of[6], (GROUPS, D, 2, FF), ((0, 16), (1, 16)), -0.2, 0.2)), 0.25, 4.0)
    outer_params = noise(streams_of[7], (D, 2, FF), 1.0, 6.0, ((0, 16),), jnp.float32)
    momentum = noise(streams_of[8], (D, 2, FF), 0.5, 3.0, ((0, 16),), jnp.float32)
    return dict(frames=frames, cotangent=cotangent, mix_partner=mix_partner, lengths=lengths, inner_params=inner_params, first_moment=first_moment, second_moment=second_moment, outer_params=outer_params, momentum=momentum)


beta_one = 0.9
beta_two = 0.98
inner_rate = 0.08
decay_rate = 0.01
adam_eps = 1e-06
outer_rate = 0.7
nesterov_mu = 0.9
norm_eps = 1e-05
mix_weight = 0.5
inv_root_two = 0.7071067811865476
inv_root_tau = 0.3989422804014327
correction_one = 1.0 - beta_one ** 500.0
correction_two = 1.0 - beta_two ** 500.0

def gelu_parts(values):
    cumulative = 0.5 * (1.0 + jax.scipy.special.erf(values * inv_root_two))
    density = jnp.exp(-0.5 * values * values) * inv_root_tau
    return (values * cumulative, cumulative + values * density)

def normalize(mixed_rows):
    centre = lax.optimization_barrier(jnp.mean(mixed_rows, axis=-1, keepdims=True))
    shifted = mixed_rows - centre
    spread = lax.optimization_barrier(jnp.mean(shifted * shifted, axis=-1, keepdims=True))
    return (shifted * lax.rsqrt(spread + norm_eps)).astype(jnp.bfloat16)

def reference(frames, cotangent, mix_partner, lengths, inner_params, first_moment, second_moment, outer_params, momentum):
    utt_count = TOK_DEV // FR
    blocks = frames.reshape(GROUPS, N_FSDP, utt_count, FR, D).astype(jnp.float32)
    partner_index = mix_partner.reshape(GROUPS, N_FSDP, utt_count).astype(jnp.int32)
    partner_rows = jnp.take_along_axis(blocks, partner_index[:, :, :, None, None], axis=2)
    mixed_rows = blocks + mix_weight * partner_rows
    normed = normalize(mixed_rows).reshape(GROUPS, N_FSDP, TOK_DEV, D)
    offsets = lax.broadcasted_iota(jnp.int32, (FR,), 0)
    keep_mask = offsets[None, None, None, :] < lengths.reshape(GROUPS, N_FSDP, utt_count)[:, :, :, None]
    keep_mask = keep_mask.reshape(GROUPS, N_FSDP, TOK_DEV, 1).astype(jnp.bfloat16)
    masked_grad = cotangent.reshape(GROUPS, N_FSDP, TOK_DEV, D) * keep_mask

    def group_step(operands):
        normed_rows, grad_rows, params, moment_rows, second_rows = operands
        flat_normed = normed_rows.reshape(-1, D)
        flat_grad = grad_rows.reshape(-1, D)
        pre_act = jnp.dot(flat_normed, params[:, 0, :], preferred_element_type=jnp.float32) * D ** (-0.5)
        back_grad = jnp.dot(flat_grad, params[:, 1, :], preferred_element_type=jnp.float32) * FF ** (-0.5)
        activation, derivative = gelu_parts(pre_act)
        activation = activation.astype(jnp.bfloat16).reshape(N_FSDP, TOK_DEV, FF)
        hidden_grad = (back_grad * derivative).astype(jnp.bfloat16).reshape(N_FSDP, TOK_DEV, FF)
        grad_in = jnp.einsum('btd,btf->bdf', normed_rows.astype(jnp.float32), hidden_grad.astype(jnp.float32)) * D ** (-0.5)
        grad_out = jnp.einsum('btd,btf->bdf', grad_rows.astype(jnp.float32), activation.astype(jnp.float32)) * FF ** (-0.5)
        partials = jnp.stack((grad_in, grad_out), axis=2).astype(jnp.bfloat16)
        partials = lax.optimization_barrier(partials).astype(jnp.float32)
        gradients = lax.optimization_barrier(jnp.sum(partials, axis=0))
        new_moment = beta_one * moment_rows + (1.0 - beta_one) * gradients
        new_second = beta_two * second_rows + (1.0 - beta_two) * gradients * gradients
        update = new_moment / correction_one / (jnp.sqrt(new_second / correction_two) + adam_eps)
        current = params.astype(jnp.float32)
        stepped = current - inner_rate * (update + decay_rate * current)
        return (new_moment, outer_params - stepped)
    new_moment, pseudo = lax.map(group_step, (normed, masked_grad, inner_params, first_moment, second_moment))
    average = lax.optimization_barrier(jnp.sum(pseudo, axis=0)) * (1.0 / GROUPS)
    new_momentum = nesterov_mu * momentum + average
    new_outer = outer_params - outer_rate * (average + nesterov_mu * new_momentum)
    return (new_moment, new_outer, new_momentum)
```

```python
import jax
import jax.numpy as jnp
from jax import lax
from jax.sharding import Mesh, PartitionSpec as P

beta_one = 0.9
beta_two = 0.98
inner_rate = 0.08
decay_rate = 0.01
adam_eps = 1e-06
outer_rate = 0.7
nesterov_mu = 0.9
norm_eps = 1e-05
mix_weight = 0.5
inv_root_two = 0.7071067811865476
inv_root_tau = 0.3989422804014327
correction_one = 1.0 - beta_one**500.0
correction_two = 1.0 - beta_two**500.0

GROUP_PARTS = (("gz", 4), ("gy", 4))
FSDP_PARTS = (("fx", 4), ("fz", 2), ("fc", 2))
GROUP_AXES = tuple(name for name, _ in GROUP_PARTS)
FSDP_AXES = tuple(name for name, _ in FSDP_PARTS)
GATHER_ORDER = ("fz", "fx", "fc")


def gelu_parts(values):
    cumulative = 0.5 * (1.0 + jax.scipy.special.erf(values * inv_root_two))
    density = jnp.exp(-0.5 * values * values) * inv_root_tau
    return (values * cumulative, cumulative + values * density)


def normalize(mixed_rows):
    centre = jnp.mean(mixed_rows, axis=-1, keepdims=True)
    shifted = mixed_rows - centre
    spread = jnp.mean(shifted * shifted, axis=-1, keepdims=True)
    return (shifted * lax.rsqrt(spread + norm_eps)).astype(jnp.bfloat16)


def gathered_order(columns):
    sizes = dict(FSDP_PARTS)
    rows = columns.shape[0]
    local = columns.shape[1] // (sizes["fx"] * sizes["fz"] * sizes["fc"])
    split = columns.reshape(rows, sizes["fx"], sizes["fz"], sizes["fc"], local)
    position = {"fx": 1, "fz": 2, "fc": 3}
    order = (0,) + tuple(position[name] for name in reversed(GATHER_ORDER)) + (4,)
    return jnp.transpose(split, order).reshape(columns.shape)


def gather_rows(block):
    for name in GATHER_ORDER:
        block = lax.all_gather(block, name, axis=0, tiled=True)
    return block


def scatter_rows(block):
    for name in reversed(GATHER_ORDER):
        block = lax.psum_scatter(block, name, scatter_dimension=0, tiled=True)
    return block


def group_sum(values):
    shape = values.shape
    flat = values.reshape(-1, 128)
    for name in reversed(GROUP_AXES):
        flat = lax.psum_scatter(flat, name, scatter_dimension=0, tiled=True)
    for name in GROUP_AXES:
        flat = lax.all_gather(flat, name, axis=0, tiled=True)
    return flat.reshape(shape)


def per_device(
    frames,
    cotangent,
    mix_partner,
    lengths,
    inner_params,
    first_moment,
    second_moment,
    outer_params,
    momentum,
):
    frame_rows = frames.shape[1]
    model_width = frames.shape[2]
    utt_count = mix_partner.shape[1]
    crop_frames = frame_rows // utt_count
    hidden_width = inner_params.shape[3]
    blocks = frames[0].reshape(utt_count, crop_frames, model_width).astype(jnp.float32)
    partner_rows = jnp.take(blocks, mix_partner[0], axis=0)
    mixed_rows = blocks + mix_weight * partner_rows
    normed = normalize(mixed_rows).reshape(frame_rows, model_width)
    offsets = lax.broadcasted_iota(jnp.int32, (utt_count, crop_frames), 1)
    keep_mask = (offsets < lengths[0][:, None]).reshape(frame_rows, 1).astype(jnp.bfloat16)
    masked_grad = cotangent[0] * keep_mask
    normed = gathered_order(normed)
    masked_grad = gathered_order(masked_grad)

    w_in = gather_rows(inner_params[0, :, 0, :])
    pre_act = jnp.dot(normed, w_in, preferred_element_type=jnp.float32) * model_width ** (-0.5)
    cumulative = 0.5 * (1.0 + jax.scipy.special.erf(pre_act * inv_root_two))
    activation = (pre_act * cumulative).astype(jnp.bfloat16)
    grad_out = lax.dot_general(
        masked_grad, activation, (((0,), (0,)), ((), ())), preferred_element_type=jnp.float32
    ) * hidden_width ** (-0.5)
    grad_out = scatter_rows(grad_out.astype(jnp.bfloat16))

    w_out = gather_rows(inner_params[0, :, 1, :])
    back_grad = jnp.dot(masked_grad, w_out, preferred_element_type=jnp.float32) * hidden_width ** (-0.5)
    density = jnp.exp(-0.5 * pre_act * pre_act) * inv_root_tau
    hidden_grad = (back_grad * (cumulative + pre_act * density)).astype(jnp.bfloat16)
    grad_in = lax.dot_general(
        normed, hidden_grad, (((0,), (0,)), ((), ())), preferred_element_type=jnp.float32
    ) * model_width ** (-0.5)
    grad_in = scatter_rows(grad_in.astype(jnp.bfloat16))

    gradients = jnp.stack((grad_in, grad_out), axis=1).astype(jnp.float32)
    new_moment = beta_one * first_moment[0] + (1.0 - beta_one) * gradients
    new_second = beta_two * second_moment[0] + (1.0 - beta_two) * gradients * gradients
    update = new_moment / correction_one / (jnp.sqrt(new_second / correction_two) + adam_eps)
    current = inner_params[0].astype(jnp.float32)
    stepped = current - inner_rate * (update + decay_rate * current)
    pseudo = outer_params - stepped
    replica_count = 1
    for _, size in GROUP_PARTS:
        replica_count *= size
    totals = group_sum(pseudo)
    average = totals * (1.0 / replica_count)
    new_momentum = nesterov_mu * momentum + average
    new_outer = outer_params - outer_rate * (average + nesterov_mu * new_momentum)
    return (new_moment[None], new_outer, new_momentum)


def solution(mesh):
    sizes = tuple(size for _, size in GROUP_PARTS + FSDP_PARTS)
    split_mesh = Mesh(mesh.devices.reshape(sizes), GROUP_AXES + FSDP_AXES)
    group, fsdp = GROUP_AXES, FSDP_AXES
    in_specs = (
        P(group, fsdp, None),
        P(group, fsdp, None),
        P(group, fsdp),
        P(group, fsdp),
        P(group, fsdp, None, None),
        P(group, fsdp, None, None),
        P(group, fsdp, None, None),
        P(fsdp, None, None),
        P(fsdp, None, None),
    )
    out_specs = (P(group, fsdp, None, None), P(fsdp, None, None), P(fsdp, None, None))
    return jax.shard_map(
        per_device, mesh=split_mesh, in_specs=in_specs, out_specs=out_specs, check_vma=False
    )
```

```python
import jax
import jax.numpy as jnp
from jax import lax
from jax.sharding import Mesh, PartitionSpec as P

beta_one = 0.9
beta_two = 0.98
inner_rate = 0.08
decay_rate = 0.01
adam_eps = 1e-06
outer_rate = 0.7
nesterov_mu = 0.9
norm_eps = 1e-05
mix_weight = 0.5
inv_root_two = 0.7071067811865476
inv_root_tau = 0.3989422804014327
correction_one = 1.0 - beta_one**500.0
correction_two = 1.0 - beta_two**500.0

GROUP_PARTS = (("gz", 4), ("gy", 4))
FSDP_PARTS = (("fx", 4), ("fz", 2), ("fc", 2))
GROUP_AXES = tuple(name for name, _ in GROUP_PARTS)
FSDP_AXES = tuple(name for name, _ in FSDP_PARTS)


def gelu_parts(values):
    cumulative = 0.5 * (1.0 + jax.scipy.special.erf(values * inv_root_two))
    density = jnp.exp(-0.5 * values * values) * inv_root_tau
    return (values * cumulative, cumulative + values * density)


def normalize(mixed_rows):
    centre = jnp.mean(mixed_rows, axis=-1, keepdims=True)
    shifted = mixed_rows - centre
    spread = jnp.mean(shifted * shifted, axis=-1, keepdims=True)
    return (shifted * lax.rsqrt(spread + norm_eps)).astype(jnp.bfloat16)


def gathered_order(columns):
    sizes = dict(FSDP_PARTS)
    rows = columns.shape[0]
    local = columns.shape[1] // (sizes["fx"] * sizes["fz"] * sizes["fc"])
    split = columns.reshape(rows, sizes["fx"], sizes["fz"], sizes["fc"], local)
    split = jnp.where(lax.axis_index("fz") == 0, split, jnp.flip(split, axis=2))
    split = jnp.where(lax.axis_index("fc") == 0, split, jnp.flip(split, axis=3))
    return jnp.transpose(split, (0, 3, 1, 2, 4)).reshape(columns.shape)


def swap(block, name):
    return lax.ppermute(block, name, perm=[(0, 1), (1, 0)])


def gather_rows(block):
    block = jnp.concatenate([block, swap(block, "fz")], axis=0)
    block = lax.all_gather(block, "fx", axis=0, tiled=True)
    return jnp.concatenate([block, swap(block, "fc")], axis=0)


def scatter_rows(block):
    half = block.shape[0] // 2
    block = block[:half].astype(jnp.float32) + swap(block[half:], "fc").astype(jnp.float32)
    block = lax.psum_scatter(block.astype(jnp.bfloat16), "fx", scatter_dimension=0, tiled=True)
    half = block.shape[0] // 2
    return block[:half].astype(jnp.float32) + swap(block[half:], "fz").astype(jnp.float32)


def group_sum(values):
    shape = values.shape
    flat = values.reshape(-1, 128)
    for name in reversed(GROUP_AXES):
        flat = lax.psum_scatter(flat, name, scatter_dimension=0, tiled=True)
    for name in GROUP_AXES:
        flat = lax.all_gather(flat, name, axis=0, tiled=True)
    return flat.reshape(shape)


def per_device(
    frames,
    cotangent,
    mix_partner,
    lengths,
    inner_params,
    first_moment,
    second_moment,
    outer_params,
    momentum,
):
    frame_rows = frames.shape[1]
    model_width = frames.shape[2]
    utt_count = mix_partner.shape[1]
    crop_frames = frame_rows // utt_count
    hidden_width = inner_params.shape[3]
    blocks = frames[0].reshape(utt_count, crop_frames, model_width).astype(jnp.float32)
    partner_rows = jnp.take(blocks, mix_partner[0], axis=0)
    mixed_rows = blocks + mix_weight * partner_rows
    normed = normalize(mixed_rows).reshape(frame_rows, model_width)
    offsets = lax.broadcasted_iota(jnp.int32, (utt_count, crop_frames), 1)
    keep_mask = (offsets < lengths[0][:, None]).reshape(frame_rows, 1).astype(jnp.bfloat16)
    masked_grad = cotangent[0] * keep_mask
    normed = gathered_order(normed)
    masked_grad = gathered_order(masked_grad)

    w_in = gather_rows(inner_params[0, :, 0, :])
    pre_act = jnp.dot(normed, w_in, preferred_element_type=jnp.float32) * model_width ** (-0.5)
    cumulative = 0.5 * (1.0 + jax.scipy.special.erf(pre_act * inv_root_two))
    activation = (pre_act * cumulative).astype(jnp.bfloat16)
    grad_out = lax.dot_general(
        masked_grad, activation, (((0,), (0,)), ((), ())), preferred_element_type=jnp.float32
    ) * hidden_width ** (-0.5)
    grad_out = scatter_rows(grad_out.astype(jnp.bfloat16))

    w_out = gather_rows(inner_params[0, :, 1, :])
    back_grad = jnp.dot(masked_grad, w_out, preferred_element_type=jnp.float32) * hidden_width ** (-0.5)
    density = jnp.exp(-0.5 * pre_act * pre_act) * inv_root_tau
    hidden_grad = (back_grad * (cumulative + pre_act * density)).astype(jnp.bfloat16)
    grad_in = lax.dot_general(
        normed, hidden_grad, (((0,), (0,)), ((), ())), preferred_element_type=jnp.float32
    ) * model_width ** (-0.5)
    grad_in = scatter_rows(grad_in.astype(jnp.bfloat16))

    gradients = jnp.stack((grad_in, grad_out), axis=1).astype(jnp.float32)
    new_moment = beta_one * first_moment[0] + (1.0 - beta_one) * gradients
    new_second = beta_two * second_moment[0] + (1.0 - beta_two) * gradients * gradients
    update = new_moment / correction_one / (jnp.sqrt(new_second / correction_two) + adam_eps)
    current = inner_params[0].astype(jnp.float32)
    stepped = current - inner_rate * (update + decay_rate * current)
    pseudo = outer_params - stepped
    replica_count = 1
    for _, size in GROUP_PARTS:
        replica_count *= size
    totals = group_sum(pseudo)
    average = totals * (1.0 / replica_count)
    new_momentum = nesterov_mu * momentum + average
    new_outer = outer_params - outer_rate * (average + nesterov_mu * new_momentum)
    return (new_moment[None], new_outer, new_momentum)


def solution(mesh):
    sizes = tuple(size for _, size in GROUP_PARTS + FSDP_PARTS)
    split_mesh = Mesh(mesh.devices.reshape(sizes), GROUP_AXES + FSDP_AXES)
    group, fsdp = GROUP_AXES, FSDP_AXES
    in_specs = (
        P(group, fsdp, None),
        P(group, fsdp, None),
        P(group, fsdp),
        P(group, fsdp),
        P(group, fsdp, None, None),
        P(group, fsdp, None, None),
        P(group, fsdp, None, None),
        P(fsdp, None, None),
        P(fsdp, None, None),
    )
    out_specs = (P(group, fsdp, None, None), P(fsdp, None, None), P(fsdp, None, None))
    return jax.shard_map(
        per_device, mesh=split_mesh, in_specs=in_specs, out_specs=out_specs, check_vma=False
    )
```

```python
import jax
import jax.numpy as jnp
from jax import lax
from jax.sharding import Mesh, PartitionSpec as P

beta_one = 0.9
beta_two = 0.98
inner_rate = 0.08
decay_rate = 0.01
adam_eps = 1e-06
outer_rate = 0.7
nesterov_mu = 0.9
norm_eps = 1e-05
mix_weight = 0.5
inv_root_two = 0.7071067811865476
inv_root_tau = 0.3989422804014327
correction_one = 1.0 - beta_one**500.0
correction_two = 1.0 - beta_two**500.0

GROUP_PARTS = (("gz", 4), ("gy", 4))
FSDP_PARTS = (("fx", 4), ("fz", 2), ("fc", 2))
GROUP_AXES = tuple(name for name, _ in GROUP_PARTS)
FSDP_AXES = tuple(name for name, _ in FSDP_PARTS)


def gelu_parts(values):
    cumulative = 0.5 * (1.0 + jax.scipy.special.erf(values * inv_root_two))
    density = jnp.exp(-0.5 * values * values) * inv_root_tau
    return (values * cumulative, cumulative + values * density)


def normalize(mixed_rows):
    centre = jnp.mean(mixed_rows, axis=-1, keepdims=True)
    shifted = mixed_rows - centre
    spread = jnp.mean(shifted * shifted, axis=-1, keepdims=True)
    return (shifted * lax.rsqrt(spread + norm_eps)).astype(jnp.bfloat16)


def gathered_order(columns):
    sizes = dict(FSDP_PARTS)
    rows = columns.shape[0]
    local = columns.shape[1] // (sizes["fx"] * sizes["fz"] * sizes["fc"])
    split = columns.reshape(rows, sizes["fx"], sizes["fz"], sizes["fc"], local)
    split = jnp.where(lax.axis_index("fz") == 0, split, jnp.flip(split, axis=2))
    split = jnp.where(lax.axis_index("fc") == 0, split, jnp.flip(split, axis=3))
    return jnp.transpose(split, (0, 3, 2, 1, 4)).reshape(columns.shape)


def swap(block, name):
    return lax.ppermute(block, name, perm=[(0, 1), (1, 0)])


def gather_rows(block):
    own = lax.all_gather(block, "fx", axis=0, tiled=True)
    partner = lax.all_gather(swap(block, "fz"), "fx", axis=0, tiled=True)
    block = jnp.concatenate([own, partner], axis=0)
    return jnp.concatenate([block, swap(block, "fc")], axis=0)


def scatter_rows(block):
    half = block.shape[0] // 2
    block = block[:half].astype(jnp.float32) + swap(block[half:], "fc").astype(jnp.float32)
    block = block.astype(jnp.bfloat16)
    half = block.shape[0] // 2
    partner = lax.psum_scatter(block[half:], "fx", scatter_dimension=0, tiled=True)
    partner = swap(partner, "fz")
    own = lax.psum_scatter(block[:half], "fx", scatter_dimension=0, tiled=True)
    return own.astype(jnp.float32) + partner.astype(jnp.float32)


def exchange_add(values, name, size, stride):
    pairs = [(index, index ^ stride) for index in range(size)]
    return values + lax.ppermute(values, name, perm=pairs)


def group_sum(values):
    sizes = dict(GROUP_PARTS)
    shape = values.shape
    flat = values.reshape(-1, 128)
    flat = lax.psum_scatter(flat, "gy", scatter_dimension=0, tiled=True)
    stride = 1
    while stride < sizes["gz"]:
        flat = exchange_add(flat, "gz", sizes["gz"], stride)
        stride *= 2
    flat = lax.all_gather(flat, "gy", axis=0, tiled=True)
    return flat.reshape(shape)


def per_device(
    frames,
    cotangent,
    mix_partner,
    lengths,
    inner_params,
    first_moment,
    second_moment,
    outer_params,
    momentum,
):
    frame_rows = frames.shape[1]
    model_width = frames.shape[2]
    utt_count = mix_partner.shape[1]
    crop_frames = frame_rows // utt_count
    hidden_width = inner_params.shape[3]
    blocks = frames[0].reshape(utt_count, crop_frames, model_width).astype(jnp.float32)
    partner_rows = jnp.take(blocks, mix_partner[0], axis=0)
    mixed_rows = blocks + mix_weight * partner_rows
    normed = normalize(mixed_rows).reshape(frame_rows, model_width)
    offsets = lax.broadcasted_iota(jnp.int32, (utt_count, crop_frames), 1)
    keep_mask = (offsets < lengths[0][:, None]).reshape(frame_rows, 1).astype(jnp.bfloat16)
    masked_grad = cotangent[0] * keep_mask
    normed = gathered_order(normed)
    masked_grad = gathered_order(masked_grad)

    w_in = gather_rows(inner_params[0, :, 0, :])
    pre_act = jnp.dot(normed, w_in, preferred_element_type=jnp.float32) * model_width ** (-0.5)
    cumulative = 0.5 * (1.0 + jax.scipy.special.erf(pre_act * inv_root_two))
    activation = (pre_act * cumulative).astype(jnp.bfloat16)
    grad_out = lax.dot_general(
        masked_grad, activation, (((0,), (0,)), ((), ())), preferred_element_type=jnp.float32
    ) * hidden_width ** (-0.5)
    grad_out = scatter_rows(grad_out.astype(jnp.bfloat16))

    w_out = gather_rows(inner_params[0, :, 1, :])
    back_grad = jnp.dot(masked_grad, w_out, preferred_element_type=jnp.float32) * hidden_width ** (-0.5)
    density = jnp.exp(-0.5 * pre_act * pre_act) * inv_root_tau
    hidden_grad = (back_grad * (cumulative + pre_act * density)).astype(jnp.bfloat16)
    grad_in = lax.dot_general(
        normed, hidden_grad, (((0,), (0,)), ((), ())), preferred_element_type=jnp.float32
    ) * model_width ** (-0.5)
    grad_in = scatter_rows(grad_in.astype(jnp.bfloat16))

    gradients = jnp.stack((grad_in, grad_out), axis=1).astype(jnp.float32)
    new_moment = beta_one * first_moment[0] + (1.0 - beta_one) * gradients
    new_second = beta_two * second_moment[0] + (1.0 - beta_two) * gradients * gradients
    update = new_moment / correction_one / (jnp.sqrt(new_second / correction_two) + adam_eps)
    current = inner_params[0].astype(jnp.float32)
    stepped = current - inner_rate * (update + decay_rate * current)
    pseudo = outer_params - stepped
    replica_count = 1
    for _, size in GROUP_PARTS:
        replica_count *= size
    totals = group_sum(pseudo)
    average = totals * (1.0 / replica_count)
    new_momentum = nesterov_mu * momentum + average
    new_outer = outer_params - outer_rate * (average + nesterov_mu * new_momentum)
    return (new_moment[None], new_outer, new_momentum)


def solution(mesh):
    sizes = tuple(size for _, size in GROUP_PARTS + FSDP_PARTS)
    split_mesh = Mesh(mesh.devices.reshape(sizes), GROUP_AXES + FSDP_AXES)
    group, fsdp = GROUP_AXES, FSDP_AXES
    in_specs = (
        P(group, fsdp, None),
        P(group, fsdp, None),
        P(group, fsdp),
        P(group, fsdp),
        P(group, fsdp, None, None),
        P(group, fsdp, None, None),
        P(group, fsdp, None, None),
        P(fsdp, None, None),
        P(fsdp, None, None),
    )
    out_specs = (P(group, fsdp, None, None), P(fsdp, None, None), P(fsdp, None, None))
    return jax.shard_map(
        per_device, mesh=split_mesh, in_specs=in_specs, out_specs=out_specs, check_vma=False
    )
```

```python
import jax
import jax.numpy as jnp
from jax import lax
from jax.sharding import Mesh, PartitionSpec as P

beta_one = 0.9
beta_two = 0.98
inner_rate = 0.08
decay_rate = 0.01
adam_eps = 1e-06
outer_rate = 0.7
nesterov_mu = 0.9
norm_eps = 1e-05
mix_weight = 0.5
inv_root_two = 0.7071067811865476
inv_root_tau = 0.3989422804014327
correction_one = 1.0 - beta_one**500.0
correction_two = 1.0 - beta_two**500.0

GROUP_PARTS = (("gz", 4), ("gy", 4))
FSDP_PARTS = (("fx", 4), ("fz", 2), ("fc", 2))
GROUP_AXES = tuple(name for name, _ in GROUP_PARTS)
FSDP_AXES = tuple(name for name, _ in FSDP_PARTS)


def gelu_parts(values):
    cumulative = 0.5 * (1.0 + jax.scipy.special.erf(values * inv_root_two))
    density = jnp.exp(-0.5 * values * values) * inv_root_tau
    return (values * cumulative, cumulative + values * density)


def normalize(mixed_rows):
    centre = jnp.mean(mixed_rows, axis=-1, keepdims=True)
    shifted = mixed_rows - centre
    spread = jnp.mean(shifted * shifted, axis=-1, keepdims=True)
    return (shifted * lax.rsqrt(spread + norm_eps)).astype(jnp.bfloat16)


def gathered_order(columns):
    sizes = dict(FSDP_PARTS)
    rows = columns.shape[0]
    local = columns.shape[1] // (sizes["fx"] * sizes["fz"] * sizes["fc"])
    split = columns.reshape(rows, sizes["fx"], sizes["fz"], sizes["fc"], local)
    split = jnp.where(lax.axis_index("fz") == 0, split, jnp.flip(split, axis=2))
    split = jnp.where(lax.axis_index("fc") == 0, split, jnp.flip(split, axis=3))
    return jnp.transpose(split, (0, 3, 1, 2, 4)).reshape(columns.shape)


def swap(block, name):
    return lax.ppermute(block, name, perm=[(0, 1), (1, 0)])


def gather_rows(block):
    block = jnp.concatenate([block, swap(block, "fz")], axis=0)
    block = lax.all_gather(block, "fx", axis=0, tiled=True)
    return jnp.concatenate([block, swap(block, "fc")], axis=0)


def scatter_rows(block):
    half = block.shape[0] // 2
    block = block[:half].astype(jnp.float32) + swap(block[half:], "fc").astype(jnp.float32)
    block = lax.psum_scatter(block.astype(jnp.bfloat16), "fx", scatter_dimension=0, tiled=True)
    half = block.shape[0] // 2
    return block[:half].astype(jnp.float32) + swap(block[half:], "fz").astype(jnp.float32)


def exchange_add(values, name, size, stride):
    pairs = [(index, index ^ stride) for index in range(size)]
    return values + lax.ppermute(values, name, perm=pairs)


def group_sum(values):
    sizes = dict(GROUP_PARTS)
    shape = values.shape
    flat = values.reshape(-1, 128)
    flat = lax.psum_scatter(flat, "gy", scatter_dimension=0, tiled=True)
    stride = 1
    while stride < sizes["gz"]:
        flat = exchange_add(flat, "gz", sizes["gz"], stride)
        stride *= 2
    flat = lax.all_gather(flat, "gy", axis=0, tiled=True)
    return flat.reshape(shape)


def per_device(
    frames,
    cotangent,
    mix_partner,
    lengths,
    inner_params,
    first_moment,
    second_moment,
    outer_params,
    momentum,
):
    frame_rows = frames.shape[1]
    model_width = frames.shape[2]
    utt_count = mix_partner.shape[1]
    crop_frames = frame_rows // utt_count
    hidden_width = inner_params.shape[3]
    blocks = frames[0].reshape(utt_count, crop_frames, model_width).astype(jnp.float32)
    partner_rows = jnp.take(blocks, mix_partner[0], axis=0)
    mixed_rows = blocks + mix_weight * partner_rows
    normed = normalize(mixed_rows).reshape(frame_rows, model_width)
    offsets = lax.broadcasted_iota(jnp.int32, (utt_count, crop_frames), 1)
    keep_mask = (offsets < lengths[0][:, None]).reshape(frame_rows, 1).astype(jnp.bfloat16)
    masked_grad = cotangent[0] * keep_mask
    normed = gathered_order(normed)
    masked_grad = gathered_order(masked_grad)

    weights = gather_rows(inner_params[0])
    w_in = weights[:, 0, :]
    w_out = weights[:, 1, :]
    pre_act = jnp.dot(normed, w_in, preferred_element_type=jnp.float32) * model_width ** (-0.5)
    back_grad = jnp.dot(masked_grad, w_out, preferred_element_type=jnp.float32) * hidden_width ** (-0.5)
    activation, derivative = gelu_parts(pre_act)
    activation = activation.astype(jnp.bfloat16)
    hidden_grad = (back_grad * derivative).astype(jnp.bfloat16)
    grad_in = lax.dot_general(
        normed, hidden_grad, (((0,), (0,)), ((), ())), preferred_element_type=jnp.float32
    ) * model_width ** (-0.5)
    grad_out = lax.dot_general(
        masked_grad, activation, (((0,), (0,)), ((), ())), preferred_element_type=jnp.float32
    ) * hidden_width ** (-0.5)
    gradients = scatter_rows(jnp.stack((grad_in, grad_out), axis=1).astype(jnp.bfloat16))
    new_moment = beta_one * first_moment[0] + (1.0 - beta_one) * gradients
    new_second = beta_two * second_moment[0] + (1.0 - beta_two) * gradients * gradients
    update = new_moment / correction_one / (jnp.sqrt(new_second / correction_two) + adam_eps)
    current = inner_params[0].astype(jnp.float32)
    stepped = current - inner_rate * (update + decay_rate * current)
    pseudo = outer_params - stepped
    replica_count = 1
    for _, size in GROUP_PARTS:
        replica_count *= size
    totals = group_sum(pseudo)
    average = totals * (1.0 / replica_count)
    new_momentum = nesterov_mu * momentum + average
    new_outer = outer_params - outer_rate * (average + nesterov_mu * new_momentum)
    return (new_moment[None], new_outer, new_momentum)


def solution(mesh):
    sizes = tuple(size for _, size in GROUP_PARTS + FSDP_PARTS)
    split_mesh = Mesh(mesh.devices.reshape(sizes), GROUP_AXES + FSDP_AXES)
    group, fsdp = GROUP_AXES, FSDP_AXES
    in_specs = (
        P(group, fsdp, None),
        P(group, fsdp, None),
        P(group, fsdp),
        P(group, fsdp),
        P(group, fsdp, None, None),
        P(group, fsdp, None, None),
        P(group, fsdp, None, None),
        P(fsdp, None, None),
        P(fsdp, None, None),
    )
    out_specs = (P(group, fsdp, None, None), P(fsdp, None, None), P(fsdp, None, None))
    return jax.shard_map(
        per_device, mesh=split_mesh, in_specs=in_specs, out_specs=out_specs, check_vma=False
    )
```

```python
import jax
import jax.numpy as jnp
from jax import lax
from jax.sharding import Mesh, PartitionSpec as P

beta_one = 0.9
beta_two = 0.98
inner_rate = 0.08
decay_rate = 0.01
adam_eps = 1e-06
outer_rate = 0.7
nesterov_mu = 0.9
norm_eps = 1e-05
mix_weight = 0.5
inv_root_two = 0.7071067811865476
inv_root_tau = 0.3989422804014327
correction_one = 1.0 - beta_one**500.0
correction_two = 1.0 - beta_two**500.0

GROUP_PARTS = (("gz", 4), ("gy", 4))
FSDP_PARTS = (("fx", 4), ("fz", 2), ("fc", 2))
GROUP_AXES = tuple(name for name, _ in GROUP_PARTS)
FSDP_AXES = tuple(name for name, _ in FSDP_PARTS)


def gelu_parts(values):
    cumulative = 0.5 * (1.0 + jax.scipy.special.erf(values * inv_root_two))
    density = jnp.exp(-0.5 * values * values) * inv_root_tau
    return (values * cumulative, cumulative + values * density)


def normalize(mixed_rows):
    centre = jnp.mean(mixed_rows, axis=-1, keepdims=True)
    shifted = mixed_rows - centre
    spread = jnp.mean(shifted * shifted, axis=-1, keepdims=True)
    return (shifted * lax.rsqrt(spread + norm_eps)).astype(jnp.bfloat16)


def gathered_order(columns):
    sizes = dict(FSDP_PARTS)
    rows = columns.shape[0]
    local = columns.shape[1] // (sizes["fx"] * sizes["fz"] * sizes["fc"])
    split = columns.reshape(rows, sizes["fx"], sizes["fz"], sizes["fc"], local)
    split = jnp.where(lax.axis_index("fz") == 0, split, jnp.flip(split, axis=2))
    split = jnp.where(lax.axis_index("fc") == 0, split, jnp.flip(split, axis=3))
    return jnp.transpose(split, (0, 3, 2, 1, 4)).reshape(columns.shape)


def swap(block, name):
    return lax.ppermute(block, name, perm=[(0, 1), (1, 0)])


def gather_rows(block, prologue):
    own = lax.all_gather(block, "fx", axis=0, tiled=True)
    partner, prologue = lax.optimization_barrier((swap(block, "fz"), prologue))
    partner = lax.all_gather(partner, "fx", axis=0, tiled=True)
    block = jnp.concatenate([own, partner], axis=0)
    return jnp.concatenate([block, swap(block, "fc")], axis=0), prologue


def scatter_rows(block):
    half = block.shape[0] // 2
    block = block[:half].astype(jnp.float32) + swap(block[half:], "fc").astype(jnp.float32)
    block = block.astype(jnp.bfloat16)
    half = block.shape[0] // 2
    partner = lax.psum_scatter(block[half:], "fx", scatter_dimension=0, tiled=True)
    own, partner = lax.optimization_barrier((block[:half], partner))
    partner = swap(partner, "fz")
    own = lax.psum_scatter(own, "fx", scatter_dimension=0, tiled=True)
    return own.astype(jnp.float32) + partner.astype(jnp.float32)


def exchange_add(values, name, size, stride):
    pairs = [(index, index ^ stride) for index in range(size)]
    return values + lax.ppermute(values, name, perm=pairs)


def group_sum(values):
    sizes = dict(GROUP_PARTS)
    shape = values.shape
    flat = values.reshape(-1, 128)
    flat = lax.psum_scatter(flat, "gy", scatter_dimension=0, tiled=True)
    stride = 1
    while stride < sizes["gz"]:
        flat = exchange_add(flat, "gz", sizes["gz"], stride)
        stride *= 2
    flat = lax.all_gather(flat, "gy", axis=0, tiled=True)
    return flat.reshape(shape)


def per_device(
    frames,
    cotangent,
    mix_partner,
    lengths,
    inner_params,
    first_moment,
    second_moment,
    outer_params,
    momentum,
):
    frame_rows = frames.shape[1]
    model_width = frames.shape[2]
    utt_count = mix_partner.shape[1]
    crop_frames = frame_rows // utt_count
    hidden_width = inner_params.shape[3]
    blocks = frames[0].reshape(utt_count, crop_frames, model_width).astype(jnp.float32)
    partner_rows = jnp.take(blocks, mix_partner[0], axis=0)
    mixed_rows = blocks + mix_weight * partner_rows
    normed = normalize(mixed_rows).reshape(frame_rows, model_width)
    offsets = lax.broadcasted_iota(jnp.int32, (utt_count, crop_frames), 1)
    keep_mask = (offsets < lengths[0][:, None]).reshape(frame_rows, 1).astype(jnp.bfloat16)
    masked_grad = cotangent[0] * keep_mask
    prologue = (gathered_order(normed), gathered_order(masked_grad))
    weights, (normed, masked_grad) = gather_rows(inner_params[0], prologue)
    w_in = weights[:, 0, :]
    w_out = weights[:, 1, :]
    pre_act = jnp.dot(normed, w_in, preferred_element_type=jnp.float32) * model_width ** (-0.5)
    back_grad = jnp.dot(masked_grad, w_out, preferred_element_type=jnp.float32) * hidden_width ** (-0.5)
    activation, derivative = gelu_parts(pre_act)
    activation = activation.astype(jnp.bfloat16)
    hidden_grad = (back_grad * derivative).astype(jnp.bfloat16)
    grad_in = lax.dot_general(
        normed, hidden_grad, (((0,), (0,)), ((), ())), preferred_element_type=jnp.float32
    ) * model_width ** (-0.5)
    grad_out = lax.dot_general(
        masked_grad, activation, (((0,), (0,)), ((), ())), preferred_element_type=jnp.float32
    ) * hidden_width ** (-0.5)
    gradients = scatter_rows(jnp.stack((grad_in, grad_out), axis=1).astype(jnp.bfloat16))
    new_moment = beta_one * first_moment[0] + (1.0 - beta_one) * gradients
    new_second = beta_two * second_moment[0] + (1.0 - beta_two) * gradients * gradients
    update = new_moment / correction_one / (jnp.sqrt(new_second / correction_two) + adam_eps)
    current = inner_params[0].astype(jnp.float32)
    stepped = current - inner_rate * (update + decay_rate * current)
    pseudo = outer_params - stepped
    replica_count = 1
    for _, size in GROUP_PARTS:
        replica_count *= size
    totals = group_sum(pseudo)
    average = totals * (1.0 / replica_count)
    new_momentum = nesterov_mu * momentum + average
    new_outer = outer_params - outer_rate * (average + nesterov_mu * new_momentum)
    return (new_moment[None], new_outer, new_momentum)


def solution(mesh):
    sizes = tuple(size for _, size in GROUP_PARTS + FSDP_PARTS)
    split_mesh = Mesh(mesh.devices.reshape(sizes), GROUP_AXES + FSDP_AXES)
    group, fsdp = GROUP_AXES, FSDP_AXES
    in_specs = (
        P(group, fsdp, None),
        P(group, fsdp, None),
        P(group, fsdp),
        P(group, fsdp),
        P(group, fsdp, None, None),
        P(group, fsdp, None, None),
        P(group, fsdp, None, None),
        P(fsdp, None, None),
        P(fsdp, None, None),
    )
    out_specs = (P(group, fsdp, None, None), P(fsdp, None, None), P(fsdp, None, None))
    return jax.shard_map(
        per_device, mesh=split_mesh, in_specs=in_specs, out_specs=out_specs, check_vma=False
    )
```

```python
import jax
import jax.numpy as jnp
from jax import lax
from jax.sharding import Mesh, PartitionSpec as P

beta_one = 0.9
beta_two = 0.98
inner_rate = 0.08
decay_rate = 0.01
adam_eps = 1e-06
outer_rate = 0.7
nesterov_mu = 0.9
norm_eps = 1e-05
mix_weight = 0.5
inv_root_two = 0.7071067811865476
inv_root_tau = 0.3989422804014327
correction_one = 1.0 - beta_one**500.0
correction_two = 1.0 - beta_two**500.0

GROUP_PARTS = (("gz", 4), ("gy", 4))
FSDP_PARTS = (("fx", 4), ("fz", 2), ("fc", 2))
GROUP_AXES = tuple(name for name, _ in GROUP_PARTS)
FSDP_AXES = tuple(name for name, _ in FSDP_PARTS)


def gelu_parts(values):
    cumulative = 0.5 * (1.0 + jax.scipy.special.erf(values * inv_root_two))
    density = jnp.exp(-0.5 * values * values) * inv_root_tau
    return (values * cumulative, cumulative + values * density)


def normalize(mixed_rows):
    centre = jnp.mean(mixed_rows, axis=-1, keepdims=True)
    shifted = mixed_rows - centre
    spread = jnp.mean(shifted * shifted, axis=-1, keepdims=True)
    return (shifted * lax.rsqrt(spread + norm_eps)).astype(jnp.bfloat16)


def gathered_order(columns):
    sizes = dict(FSDP_PARTS)
    rows = columns.shape[0]
    local = columns.shape[1] // (sizes["fx"] * sizes["fz"] * sizes["fc"])
    split = columns.reshape(rows, sizes["fx"], sizes["fz"], sizes["fc"], local)
    split = jnp.where(lax.axis_index("fz") == 0, split, jnp.flip(split, axis=2))
    split = jnp.where(lax.axis_index("fc") == 0, split, jnp.flip(split, axis=3))
    return jnp.transpose(split, (0, 3, 2, 1, 4)).reshape(columns.shape)


def swap(block, name):
    return lax.ppermute(block, name, perm=[(0, 1), (1, 0)])


def gather_pieces(block, prologue):
    own = lax.all_gather(block, "fx", axis=0, tiled=True)
    partner, prologue = lax.optimization_barrier((swap(block, "fz"), prologue))
    own_sibling = swap(own, "fc")
    partner = lax.all_gather(partner, "fx", axis=0, tiled=True)
    partner_sibling = swap(partner, "fc")
    return (own, partner, own_sibling, partner_sibling), prologue


def fold_core(own, sibling):
    total = own.astype(jnp.float32) + swap(sibling, "fc").astype(jnp.float32)
    return total.astype(jnp.bfloat16)


def exchange_add(values, name, size, stride):
    pairs = [(index, index ^ stride) for index in range(size)]
    return values + lax.ppermute(values, name, perm=pairs)


def group_sum(values):
    sizes = dict(GROUP_PARTS)
    shape = values.shape
    flat = values.reshape(-1, 128)
    flat = lax.psum_scatter(flat, "gy", scatter_dimension=0, tiled=True)
    stride = 1
    while stride < sizes["gz"]:
        flat = exchange_add(flat, "gz", sizes["gz"], stride)
        stride *= 2
    flat = lax.all_gather(flat, "gy", axis=0, tiled=True)
    return flat.reshape(shape)


def per_device(
    frames,
    cotangent,
    mix_partner,
    lengths,
    inner_params,
    first_moment,
    second_moment,
    outer_params,
    momentum,
):
    frame_rows = frames.shape[1]
    model_width = frames.shape[2]
    utt_count = mix_partner.shape[1]
    crop_frames = frame_rows // utt_count
    hidden_width = inner_params.shape[3]
    blocks = frames[0].reshape(utt_count, crop_frames, model_width).astype(jnp.float32)
    partner_rows = jnp.take(blocks, mix_partner[0], axis=0)
    mixed_rows = blocks + mix_weight * partner_rows
    normed = normalize(mixed_rows).reshape(frame_rows, model_width)
    offsets = lax.broadcasted_iota(jnp.int32, (utt_count, crop_frames), 1)
    keep_mask = (offsets < lengths[0][:, None]).reshape(frame_rows, 1).astype(jnp.bfloat16)
    masked_grad = cotangent[0] * keep_mask
    prologue = (gathered_order(normed), gathered_order(masked_grad))
    pieces, (normed, masked_grad) = gather_pieces(inner_params[0], prologue)
    width = pieces[0].shape[0]
    normed_parts = [normed[:, i * width : (i + 1) * width] for i in range(len(pieces))]
    grad_parts = [masked_grad[:, i * width : (i + 1) * width] for i in range(len(pieces))]
    pre_sum = None
    back_sum = None
    for normed_part, grad_part, piece in zip(normed_parts, grad_parts, pieces):
        pre_term = jnp.dot(normed_part, piece[:, 0, :], preferred_element_type=jnp.float32)
        back_term = jnp.dot(grad_part, piece[:, 1, :], preferred_element_type=jnp.float32)
        pre_sum = pre_term if pre_sum is None else pre_sum + pre_term
        back_sum = back_term if back_sum is None else back_sum + back_term
    pre_act = pre_sum * model_width ** (-0.5)
    back_grad = back_sum * hidden_width ** (-0.5)
    activation, derivative = gelu_parts(pre_act)
    activation = activation.astype(jnp.bfloat16)
    hidden_grad = (back_grad * derivative).astype(jnp.bfloat16)

    def piece_grad(index):
        grad_in = lax.dot_general(
            normed_parts[index], hidden_grad, (((0,), (0,)), ((), ())),
            preferred_element_type=jnp.float32,
        ) * model_width ** (-0.5)
        grad_out = lax.dot_general(
            grad_parts[index], activation, (((0,), (0,)), ((), ())),
            preferred_element_type=jnp.float32,
        ) * hidden_width ** (-0.5)
        return jnp.stack((grad_in, grad_out), axis=1).astype(jnp.bfloat16)

    partner_rows = fold_core(piece_grad(1), piece_grad(3))
    partner_rows = lax.psum_scatter(partner_rows, "fx", scatter_dimension=0, tiled=True)
    own_rows = fold_core(piece_grad(0), piece_grad(2))
    own_rows, partner_rows = lax.optimization_barrier((own_rows, partner_rows))
    partner_rows = swap(partner_rows, "fz")
    own_rows = lax.psum_scatter(own_rows, "fx", scatter_dimension=0, tiled=True)
    gradients = own_rows.astype(jnp.float32) + partner_rows.astype(jnp.float32)
    new_moment = beta_one * first_moment[0] + (1.0 - beta_one) * gradients
    new_second = beta_two * second_moment[0] + (1.0 - beta_two) * gradients * gradients
    update = new_moment / correction_one / (jnp.sqrt(new_second / correction_two) + adam_eps)
    current = inner_params[0].astype(jnp.float32)
    stepped = current - inner_rate * (update + decay_rate * current)
    pseudo = outer_params - stepped
    replica_count = 1
    for _, size in GROUP_PARTS:
        replica_count *= size
    totals = group_sum(pseudo)
    average = totals * (1.0 / replica_count)
    new_momentum = nesterov_mu * momentum + average
    new_outer = outer_params - outer_rate * (average + nesterov_mu * new_momentum)
    return (new_moment[None], new_outer, new_momentum)


def solution(mesh):
    sizes = tuple(size for _, size in GROUP_PARTS + FSDP_PARTS)
    split_mesh = Mesh(mesh.devices.reshape(sizes), GROUP_AXES + FSDP_AXES)
    group, fsdp = GROUP_AXES, FSDP_AXES
    in_specs = (
        P(group, fsdp, None),
        P(group, fsdp, None),
        P(group, fsdp),
        P(group, fsdp),
        P(group, fsdp, None, None),
        P(group, fsdp, None, None),
        P(group, fsdp, None, None),
        P(fsdp, None, None),
        P(fsdp, None, None),
    )
    out_specs = (P(group, fsdp, None, None), P(fsdp, None, None), P(fsdp, None, None))
    return jax.shard_map(
        per_device, mesh=split_mesh, in_specs=in_specs, out_specs=out_specs, check_vma=False
    )
```

```python
import jax
import jax.numpy as jnp
from jax import lax
from jax.experimental import pallas as pl
from jax.experimental.pallas import tpu as pltpu
from jax.sharding import Mesh, PartitionSpec as P

MESH = pl.DeviceIdType.MESH

beta_one = 0.9
beta_two = 0.98
inner_rate = 0.08
decay_rate = 0.01
adam_eps = 1e-06
outer_rate = 0.7
nesterov_mu = 0.9
norm_eps = 1e-05
mix_weight = 0.5
inv_root_two = 0.7071067811865476
inv_root_tau = 0.3989422804014327
correction_one = 1.0 - beta_one**500.0
correction_two = 1.0 - beta_two**500.0

GROUP_PARTS = (("gz", 4), ("gy", 4))
FSDP_PARTS = (("fx", 4), ("fz", 2), ("fc", 2))
GROUP_AXES = tuple(name for name, _ in GROUP_PARTS)
FSDP_AXES = tuple(name for name, _ in FSDP_PARTS)


def gelu_parts(values):
    cumulative = 0.5 * (1.0 + jax.scipy.special.erf(values * inv_root_two))
    density = jnp.exp(-0.5 * values * values) * inv_root_tau
    return (values * cumulative, cumulative + values * density)


def normalize(mixed_rows):
    centre = jnp.mean(mixed_rows, axis=-1, keepdims=True)
    shifted = mixed_rows - centre
    spread = jnp.mean(shifted * shifted, axis=-1, keepdims=True)
    return (shifted * lax.rsqrt(spread + norm_eps)).astype(jnp.bfloat16)


def gathered_order(columns):
    sizes = dict(FSDP_PARTS)
    rows = columns.shape[0]
    local = columns.shape[1] // (sizes["fx"] * sizes["fz"] * sizes["fc"])
    split = columns.reshape(rows, sizes["fx"], sizes["fz"], sizes["fc"], local)
    split = jnp.where(lax.axis_index("fz") == 0, split, jnp.flip(split, axis=2))
    split = jnp.where(lax.axis_index("fc") == 0, split, jnp.flip(split, axis=3))
    return jnp.transpose(split, (0, 3, 2, 1, 4)).reshape(columns.shape)


def swap(block, name):
    return lax.ppermute(block, name, perm=[(0, 1), (1, 0)])


def gather_pieces(block, prologue):
    own = lax.all_gather(block, "fx", axis=0, tiled=True)
    partner, prologue = lax.optimization_barrier((swap(block, "fz"), prologue))
    own_sibling = swap(own, "fc")
    partner = lax.all_gather(partner, "fx", axis=0, tiled=True)
    partner_sibling = swap(partner, "fc")
    return (own, partner, own_sibling, partner_sibling), prologue


def fold_core(own, sibling):
    total = own.astype(jnp.float32) + swap(sibling, "fc").astype(jnp.float32)
    return total.astype(jnp.bfloat16)


def group_sum_kernel(x_ref, out_ref, recv, send_sem, recv_sem, back_sem, arrive_sem):
    ny = dict(GROUP_PARTS)["gy"]
    n = recv.shape[0]
    me = lax.axis_index("gz") * ny + lax.axis_index("gy")

    def member(index):
        return {"gz": index // ny, "gy": index % ny}

    barrier = pltpu.get_barrier_semaphore()
    for step in range(1, n):
        pl.semaphore_signal(
            barrier, inc=1, device_id=member((me + step) % n), device_id_type=MESH
        )
    pl.semaphore_wait(barrier, n - 1)

    scatter = []
    for step in range(1, n):
        peer = (me + step) % n
        copy = pltpu.make_async_remote_copy(
            src_ref=x_ref.at[peer],
            dst_ref=recv.at[me],
            send_sem=send_sem.at[peer],
            recv_sem=recv_sem.at[me],
            device_id=member(peer),
            device_id_type=MESH,
        )
        copy.start()
        scatter.append(copy)
    recv[me] = x_ref[me]
    for step in range(1, n):
        sender = (me + n - step) % n
        pltpu.make_async_remote_copy(
            src_ref=x_ref.at[sender],
            dst_ref=recv.at[sender],
            send_sem=send_sem.at[sender],
            recv_sem=recv_sem.at[sender],
            device_id=member(sender),
            device_id_type=MESH,
        ).wait_recv()
    total = recv[0].astype(jnp.float32)
    for index in range(1, n):
        total = total + recv[index].astype(jnp.float32)
    out_ref[me] = total.astype(out_ref.dtype)

    gather = []
    for step in range(1, n):
        peer = (me + step) % n
        copy = pltpu.make_async_remote_copy(
            src_ref=out_ref.at[me],
            dst_ref=out_ref.at[me],
            send_sem=back_sem.at[peer],
            recv_sem=arrive_sem.at[me],
            device_id=member(peer),
            device_id_type=MESH,
        )
        copy.start()
        gather.append(copy)
    for step in range(1, n):
        sender = (me + n - step) % n
        pltpu.make_async_remote_copy(
            src_ref=out_ref.at[me],
            dst_ref=out_ref.at[sender],
            send_sem=back_sem.at[sender],
            recv_sem=arrive_sem.at[sender],
            device_id=member(sender),
            device_id_type=MESH,
        ).wait_recv()
    for copy in scatter + gather:
        copy.wait_send()


def group_sum_update(values):
    n = 1
    for _, size in GROUP_PARTS:
        n *= size
    shape = values.shape
    blocks = values.astype(jnp.bfloat16).reshape(n, -1, 128)
    rows = blocks.shape[1]
    padded = -(-rows // 16) * 16
    blocks = jnp.pad(blocks, ((0, 0), (0, padded - rows), (0, 0)))
    semaphores = [pltpu.SemaphoreType.DMA((n,)) for _ in range(4)]
    summed = pl.pallas_call(
        group_sum_kernel,
        out_shape=jax.ShapeDtypeStruct(blocks.shape, jnp.bfloat16),
        in_specs=[pl.BlockSpec(memory_space=pltpu.VMEM)],
        out_specs=pl.BlockSpec(memory_space=pltpu.VMEM),
        scratch_shapes=[pltpu.VMEM(blocks.shape, jnp.bfloat16)] + semaphores,
        compiler_params=pltpu.CompilerParams(collective_id=0, has_side_effects=True),
    )(blocks)
    return summed[:, :rows].astype(jnp.float32).reshape(shape)


def exchange_add(values, name, size, stride):
    pairs = [(index, index ^ stride) for index in range(size)]
    return values + lax.ppermute(values, name, perm=pairs)


def group_sum_early(values):
    shape = values.shape
    flat = values.reshape(-1, 128)
    for name, size in reversed(GROUP_PARTS):
        stride = 1
        while stride < size:
            flat = exchange_add(flat, name, size, stride)
            stride *= 2
    return flat.reshape(shape)


def per_device(
    frames,
    cotangent,
    mix_partner,
    lengths,
    inner_params,
    first_moment,
    second_moment,
    outer_params,
    momentum,
):
    frame_rows = frames.shape[1]
    model_width = frames.shape[2]
    utt_count = mix_partner.shape[1]
    crop_frames = frame_rows // utt_count
    hidden_width = inner_params.shape[3]
    blocks = frames[0].reshape(utt_count, crop_frames, model_width).astype(jnp.float32)
    partner_rows = jnp.take(blocks, mix_partner[0], axis=0)
    mixed_rows = blocks + mix_weight * partner_rows
    normed = normalize(mixed_rows).reshape(frame_rows, model_width)
    offsets = lax.broadcasted_iota(jnp.int32, (utt_count, crop_frames), 1)
    keep_mask = (offsets < lengths[0][:, None]).reshape(frame_rows, 1).astype(jnp.bfloat16)
    masked_grad = cotangent[0] * keep_mask
    prologue = (gathered_order(normed), gathered_order(masked_grad))
    pieces, (normed, masked_grad) = gather_pieces(inner_params[0], prologue)
    width = pieces[0].shape[0]
    normed_parts = [normed[:, i * width : (i + 1) * width] for i in range(len(pieces))]
    grad_parts = [masked_grad[:, i * width : (i + 1) * width] for i in range(len(pieces))]
    pre_sum = None
    back_sum = None
    for normed_part, grad_part, piece in zip(normed_parts, grad_parts, pieces):
        pre_term = jnp.dot(normed_part, piece[:, 0, :], preferred_element_type=jnp.float32)
        back_term = jnp.dot(grad_part, piece[:, 1, :], preferred_element_type=jnp.float32)
        pre_sum = pre_term if pre_sum is None else pre_sum + pre_term
        back_sum = back_term if back_sum is None else back_sum + back_term
    pre_act = pre_sum * model_width ** (-0.5)
    back_grad = back_sum * hidden_width ** (-0.5)
    activation, derivative = gelu_parts(pre_act)
    activation = activation.astype(jnp.bfloat16)
    hidden_grad = (back_grad * derivative).astype(jnp.bfloat16)

    def piece_grad(index):
        grad_in = lax.dot_general(
            normed_parts[index], hidden_grad, (((0,), (0,)), ((), ())),
            preferred_element_type=jnp.float32,
        ) * model_width ** (-0.5)
        grad_out = lax.dot_general(
            grad_parts[index], activation, (((0,), (0,)), ((), ())),
            preferred_element_type=jnp.float32,
        ) * hidden_width ** (-0.5)
        return jnp.stack((grad_in, grad_out), axis=1).astype(jnp.bfloat16)

    current = inner_params[0].astype(jnp.float32)
    settled = group_sum_early(outer_params - (1.0 - inner_rate * decay_rate) * current)
    partner_rows, settled = lax.optimization_barrier(
        (fold_core(piece_grad(1), piece_grad(3)), settled)
    )
    partner_rows = lax.psum_scatter(partner_rows, "fx", scatter_dimension=0, tiled=True)
    own_rows = fold_core(piece_grad(0), piece_grad(2))
    own_rows, partner_rows = lax.optimization_barrier((own_rows, partner_rows))
    partner_rows = swap(partner_rows, "fz")
    own_rows = lax.psum_scatter(own_rows, "fx", scatter_dimension=0, tiled=True)
    gradients = own_rows.astype(jnp.float32) + partner_rows.astype(jnp.float32)
    new_moment = beta_one * first_moment[0] + (1.0 - beta_one) * gradients
    new_second = beta_two * second_moment[0] + (1.0 - beta_two) * gradients * gradients
    update = new_moment / correction_one / (jnp.sqrt(new_second / correction_two) + adam_eps)
    replica_count = 1
    for _, size in GROUP_PARTS:
        replica_count *= size
    totals = settled + inner_rate * group_sum_update(update)
    average = totals * (1.0 / replica_count)
    new_momentum = nesterov_mu * momentum + average
    new_outer = outer_params - outer_rate * (average + nesterov_mu * new_momentum)
    return (new_moment[None], new_outer, new_momentum)


def solution(mesh):
    sizes = tuple(size for _, size in GROUP_PARTS + FSDP_PARTS)
    split_mesh = Mesh(mesh.devices.reshape(sizes), GROUP_AXES + FSDP_AXES)
    group, fsdp = GROUP_AXES, FSDP_AXES
    in_specs = (
        P(group, fsdp, None),
        P(group, fsdp, None),
        P(group, fsdp),
        P(group, fsdp),
        P(group, fsdp, None, None),
        P(group, fsdp, None, None),
        P(group, fsdp, None, None),
        P(fsdp, None, None),
        P(fsdp, None, None),
    )
    out_specs = (P(group, fsdp, None, None), P(fsdp, None, None), P(fsdp, None, None))
    return jax.shard_map(
        per_device, mesh=split_mesh, in_specs=in_specs, out_specs=out_specs, check_vma=False
    )
```

```python
import jax
import jax.numpy as jnp
from jax import lax
from jax.experimental import pallas as pl
from jax.experimental.pallas import tpu as pltpu
from jax.sharding import Mesh, PartitionSpec as P

MESH = pl.DeviceIdType.MESH

beta_one = 0.9
beta_two = 0.98
inner_rate = 0.08
decay_rate = 0.01
adam_eps = 1e-06
outer_rate = 0.7
nesterov_mu = 0.9
norm_eps = 1e-05
mix_weight = 0.5
inv_root_two = 0.7071067811865476
inv_root_tau = 0.3989422804014327
correction_one = 1.0 - beta_one**500.0
correction_two = 1.0 - beta_two**500.0

GROUP_PARTS = (("gz", 4), ("gy", 4))
FSDP_PARTS = (("fx", 4), ("fz", 2), ("fc", 2))
GROUP_AXES = tuple(name for name, _ in GROUP_PARTS)
FSDP_AXES = tuple(name for name, _ in FSDP_PARTS)


def gelu_parts(values):
    cumulative = 0.5 * (1.0 + jax.scipy.special.erf(values * inv_root_two))
    density = jnp.exp(-0.5 * values * values) * inv_root_tau
    return (values * cumulative, cumulative + values * density)


def normalize(mixed_rows):
    centre = jnp.mean(mixed_rows, axis=-1, keepdims=True)
    shifted = mixed_rows - centre
    spread = jnp.mean(shifted * shifted, axis=-1, keepdims=True)
    return (shifted * lax.rsqrt(spread + norm_eps)).astype(jnp.bfloat16)


def gathered_order(columns):
    sizes = dict(FSDP_PARTS)
    rows = columns.shape[0]
    local = columns.shape[1] // (sizes["fx"] * sizes["fz"] * sizes["fc"])
    split = columns.reshape(rows, sizes["fx"], sizes["fz"], sizes["fc"], local)
    split = jnp.where(lax.axis_index("fz") == 0, split, jnp.flip(split, axis=2))
    split = jnp.where(lax.axis_index("fc") == 0, split, jnp.flip(split, axis=3))
    return jnp.transpose(split, (0, 3, 2, 1, 4)).reshape(columns.shape)


def swap(block, name):
    return lax.ppermute(block, name, perm=[(0, 1), (1, 0)])


def gather_pieces(block, prologue):
    own = lax.all_gather(block, "fx", axis=0, tiled=True)
    partner, prologue = lax.optimization_barrier((swap(block, "fz"), prologue))
    own_sibling = swap(own, "fc")
    partner = lax.all_gather(partner, "fx", axis=0, tiled=True)
    partner_sibling = swap(partner, "fc")
    return (own, partner, own_sibling, partner_sibling), prologue


def fold_core(own, sibling):
    total = own.astype(jnp.float32) + swap(sibling, "fc").astype(jnp.float32)
    return total.astype(jnp.bfloat16)


def group_sum_kernel(x_ref, out_ref, recv, send_sem, recv_sem, back_sem, arrive_sem):
    ny = dict(GROUP_PARTS)["gy"]
    n = recv.shape[0]
    me = lax.axis_index("gz") * ny + lax.axis_index("gy")

    def member(index):
        return {"gz": index // ny, "gy": index % ny}

    barrier = pltpu.get_barrier_semaphore()
    for step in range(1, n):
        pl.semaphore_signal(
            barrier, inc=1, device_id=member((me + step) % n), device_id_type=MESH
        )
    pl.semaphore_wait(barrier, n - 1)

    scatter = []
    for step in range(1, n):
        peer = (me + step) % n
        copy = pltpu.make_async_remote_copy(
            src_ref=x_ref.at[peer],
            dst_ref=recv.at[me],
            send_sem=send_sem.at[peer],
            recv_sem=recv_sem.at[me],
            device_id=member(peer),
            device_id_type=MESH,
        )
        copy.start()
        scatter.append(copy)
    recv[me] = x_ref[me]
    for step in range(1, n):
        sender = (me + n - step) % n
        pltpu.make_async_remote_copy(
            src_ref=x_ref.at[sender],
            dst_ref=recv.at[sender],
            send_sem=send_sem.at[sender],
            recv_sem=recv_sem.at[sender],
            device_id=member(sender),
            device_id_type=MESH,
        ).wait_recv()
    total = recv[0].astype(jnp.float32)
    for index in range(1, n):
        total = total + recv[index].astype(jnp.float32)
    out_ref[me] = total.astype(out_ref.dtype)

    gather = []
    for step in range(1, n):
        peer = (me + step) % n
        copy = pltpu.make_async_remote_copy(
            src_ref=out_ref.at[me],
            dst_ref=out_ref.at[me],
            send_sem=back_sem.at[peer],
            recv_sem=arrive_sem.at[me],
            device_id=member(peer),
            device_id_type=MESH,
        )
        copy.start()
        gather.append(copy)
    for step in range(1, n):
        sender = (me + n - step) % n
        pltpu.make_async_remote_copy(
            src_ref=out_ref.at[me],
            dst_ref=out_ref.at[sender],
            send_sem=back_sem.at[sender],
            recv_sem=arrive_sem.at[sender],
            device_id=member(sender),
            device_id_type=MESH,
        ).wait_recv()
    for copy in scatter + gather:
        copy.wait_send()


def group_sum(values, out_dtype, collective_id):
    n = 1
    for _, size in GROUP_PARTS:
        n *= size
    shape = values.shape
    blocks = values.astype(jnp.bfloat16).reshape(n, -1, 128)
    rows = blocks.shape[1]
    padded = -(-rows // 16) * 16
    blocks = jnp.pad(blocks, ((0, 0), (0, padded - rows), (0, 0)))
    semaphores = [pltpu.SemaphoreType.DMA((n,)) for _ in range(4)]
    summed = pl.pallas_call(
        group_sum_kernel,
        out_shape=jax.ShapeDtypeStruct(blocks.shape, out_dtype),
        in_specs=[pl.BlockSpec(memory_space=pltpu.VMEM)],
        out_specs=pl.BlockSpec(memory_space=pltpu.VMEM),
        scratch_shapes=[pltpu.VMEM(blocks.shape, jnp.bfloat16)] + semaphores,
        compiler_params=pltpu.CompilerParams(
            collective_id=collective_id, has_side_effects=True
        ),
    )(blocks)
    return summed[:, :rows].astype(jnp.float32).reshape(shape)


def per_device(
    frames,
    cotangent,
    mix_partner,
    lengths,
    inner_params,
    first_moment,
    second_moment,
    outer_params,
    momentum,
):
    frame_rows = frames.shape[1]
    model_width = frames.shape[2]
    utt_count = mix_partner.shape[1]
    crop_frames = frame_rows // utt_count
    hidden_width = inner_params.shape[3]
    blocks = frames[0].reshape(utt_count, crop_frames, model_width).astype(jnp.float32)
    partner_rows = jnp.take(blocks, mix_partner[0], axis=0)
    mixed_rows = blocks + mix_weight * partner_rows
    normed = normalize(mixed_rows).reshape(frame_rows, model_width)
    offsets = lax.broadcasted_iota(jnp.int32, (utt_count, crop_frames), 1)
    keep_mask = (offsets < lengths[0][:, None]).reshape(frame_rows, 1).astype(jnp.bfloat16)
    masked_grad = cotangent[0] * keep_mask
    prologue = (gathered_order(normed), gathered_order(masked_grad))
    pieces, (normed, masked_grad) = gather_pieces(inner_params[0], prologue)
    width = pieces[0].shape[0]
    normed_parts = [normed[:, i * width : (i + 1) * width] for i in range(len(pieces))]
    grad_parts = [masked_grad[:, i * width : (i + 1) * width] for i in range(len(pieces))]
    pre_sum = None
    back_sum = None
    for normed_part, grad_part, piece in zip(normed_parts, grad_parts, pieces):
        pre_term = jnp.dot(normed_part, piece[:, 0, :], preferred_element_type=jnp.float32)
        back_term = jnp.dot(grad_part, piece[:, 1, :], preferred_element_type=jnp.float32)
        pre_sum = pre_term if pre_sum is None else pre_sum + pre_term
        back_sum = back_term if back_sum is None else back_sum + back_term
    pre_act = pre_sum * model_width ** (-0.5)
    back_grad = back_sum * hidden_width ** (-0.5)
    activation, derivative = gelu_parts(pre_act)
    activation = activation.astype(jnp.bfloat16)
    hidden_grad = (back_grad * derivative).astype(jnp.bfloat16)

    def piece_grad(index):
        grad_in = lax.dot_general(
            normed_parts[index], hidden_grad, (((0,), (0,)), ((), ())),
            preferred_element_type=jnp.float32,
        ) * model_width ** (-0.5)
        grad_out = lax.dot_general(
            grad_parts[index], activation, (((0,), (0,)), ((), ())),
            preferred_element_type=jnp.float32,
        ) * hidden_width ** (-0.5)
        return jnp.stack((grad_in, grad_out), axis=1).astype(jnp.bfloat16)

    partner_rows = fold_core(piece_grad(1), piece_grad(3))
    partner_rows = lax.psum_scatter(partner_rows, "fx", scatter_dimension=0, tiled=True)
    own_rows = fold_core(piece_grad(0), piece_grad(2))
    own_rows, weights = lax.optimization_barrier((own_rows, inner_params[0]))
    weight_sum = group_sum(weights, jnp.float32, 0)
    own_rows, partner_rows, weight_sum = lax.optimization_barrier(
        (own_rows, partner_rows, weight_sum)
    )
    partner_rows = swap(partner_rows, "fz")
    own_rows = lax.psum_scatter(own_rows, "fx", scatter_dimension=0, tiled=True)
    gradients = own_rows.astype(jnp.float32) + partner_rows.astype(jnp.float32)
    new_moment = beta_one * first_moment[0] + (1.0 - beta_one) * gradients
    new_second = beta_two * second_moment[0] + (1.0 - beta_two) * gradients * gradients
    update = new_moment / correction_one / (jnp.sqrt(new_second / correction_two) + adam_eps)
    replica_count = 1
    for _, size in GROUP_PARTS:
        replica_count *= size
    update_sum = group_sum(update, jnp.bfloat16, 1)
    totals = (
        replica_count * outer_params
        - (1.0 - inner_rate * decay_rate) * weight_sum
        + inner_rate * update_sum
    )
    average = totals * (1.0 / replica_count)
    new_momentum = nesterov_mu * momentum + average
    new_outer = outer_params - outer_rate * (average + nesterov_mu * new_momentum)
    return (new_moment[None], new_outer, new_momentum)


def solution(mesh):
    sizes = tuple(size for _, size in GROUP_PARTS + FSDP_PARTS)
    split_mesh = Mesh(mesh.devices.reshape(sizes), GROUP_AXES + FSDP_AXES)
    group, fsdp = GROUP_AXES, FSDP_AXES
    in_specs = (
        P(group, fsdp, None),
        P(group, fsdp, None),
        P(group, fsdp),
        P(group, fsdp),
        P(group, fsdp, None, None),
        P(group, fsdp, None, None),
        P(group, fsdp, None, None),
        P(fsdp, None, None),
        P(fsdp, None, None),
    )
    out_specs = (P(group, fsdp, None, None), P(fsdp, None, None), P(fsdp, None, None))
    return jax.shard_map(
        per_device, mesh=split_mesh, in_specs=in_specs, out_specs=out_specs, check_vma=False
    )
```

```python
import jax
import jax.numpy as jnp
from jax import lax
from jax.experimental import pallas as pl
from jax.experimental.pallas import tpu as pltpu
from jax.sharding import Mesh, PartitionSpec as P

MESH = pl.DeviceIdType.MESH

beta_one = 0.9
beta_two = 0.98
inner_rate = 0.08
decay_rate = 0.01
adam_eps = 1e-06
outer_rate = 0.7
nesterov_mu = 0.9
norm_eps = 1e-05
mix_weight = 0.5
inv_root_two = 0.7071067811865476
inv_root_tau = 0.3989422804014327
correction_one = 1.0 - beta_one**500.0
correction_two = 1.0 - beta_two**500.0

GROUP_PARTS = (("gz", 4), ("gy", 4))
FSDP_PARTS = (("fx", 4), ("fz", 2), ("fc", 2))
GROUP_AXES = tuple(name for name, _ in GROUP_PARTS)
FSDP_AXES = tuple(name for name, _ in FSDP_PARTS)


def gelu_parts(values):
    cumulative = 0.5 * (1.0 + jax.scipy.special.erf(values * inv_root_two))
    density = jnp.exp(-0.5 * values * values) * inv_root_tau
    return (values * cumulative, cumulative + values * density)


def normalize(mixed_rows):
    centre = jnp.mean(mixed_rows, axis=-1, keepdims=True)
    shifted = mixed_rows - centre
    spread = jnp.mean(shifted * shifted, axis=-1, keepdims=True)
    return (shifted * lax.rsqrt(spread + norm_eps)).astype(jnp.bfloat16)


def gathered_order(columns):
    sizes = dict(FSDP_PARTS)
    rows = columns.shape[0]
    local = columns.shape[1] // (sizes["fx"] * sizes["fz"] * sizes["fc"])
    split = columns.reshape(rows, sizes["fx"], sizes["fz"], sizes["fc"], local)
    split = jnp.where(lax.axis_index("fz") == 0, split, jnp.flip(split, axis=2))
    split = jnp.where(lax.axis_index("fc") == 0, split, jnp.flip(split, axis=3))
    return jnp.transpose(split, (0, 3, 2, 1, 4)).reshape(columns.shape)


def swap(block, name):
    return lax.ppermute(block, name, perm=[(0, 1), (1, 0)])


def gather_pieces(block, prologue):
    own = lax.all_gather(block, "fx", axis=0, tiled=True)
    partner, prologue = lax.optimization_barrier((swap(block, "fz"), prologue))
    own, weights = lax.optimization_barrier((own, block))
    own_sibling = swap(own, "fc")
    weight_sum = weight_group_sum(weights)
    partner = lax.all_gather(partner, "fx", axis=0, tiled=True)
    partner, weight_sum = lax.optimization_barrier((partner, weight_sum))
    partner_sibling = swap(partner, "fc")
    return (own, partner, own_sibling, partner_sibling), prologue, weight_sum


def fold_core(own, sibling):
    total = own.astype(jnp.float32) + swap(sibling, "fc").astype(jnp.float32)
    return total.astype(jnp.bfloat16)


def group_member():
    ny = dict(GROUP_PARTS)["gy"]
    me = lax.axis_index("gz") * ny + lax.axis_index("gy")

    def member(index):
        return {"gz": index // ny, "gy": index % ny}

    return me, member


def enter_group(n, me, member):
    barrier = pltpu.get_barrier_semaphore()
    for step in range(1, n):
        pl.semaphore_signal(
            barrier, inc=1, device_id=member((me + step) % n), device_id_type=MESH
        )
    pl.semaphore_wait(barrier, n - 1)


def scatter_sum(x_ref, recv, send_sem, recv_sem, me, member):
    n = recv.shape[0]
    copies = []
    for step in range(1, n):
        peer = (me + step) % n
        copy = pltpu.make_async_remote_copy(
            src_ref=x_ref.at[peer],
            dst_ref=recv.at[me],
            send_sem=send_sem.at[peer],
            recv_sem=recv_sem.at[me],
            device_id=member(peer),
            device_id_type=MESH,
        )
        copy.start()
        copies.append(copy)
    recv[me] = x_ref[me]
    for step in range(1, n):
        sender = (me + n - step) % n
        pltpu.make_async_remote_copy(
            src_ref=x_ref.at[sender],
            dst_ref=recv.at[sender],
            send_sem=send_sem.at[sender],
            recv_sem=recv_sem.at[sender],
            device_id=member(sender),
            device_id_type=MESH,
        ).wait_recv()
    total = recv[0].astype(jnp.float32)
    for index in range(1, n):
        total = total + recv[index].astype(jnp.float32)
    return copies, total


def weight_sum_kernel(x_ref, out_ref, recv, send_sem, recv_sem):
    me, member = group_member()
    enter_group(recv.shape[0], me, member)
    copies, total = scatter_sum(x_ref, recv, send_sem, recv_sem, me, member)
    out_ref[...] = total
    for copy in copies:
        copy.wait_send()


def outer_sum_kernel(
    update_ref, weight_ref, outer_ref, out_ref, recv, send_sem, recv_sem, back_sem, arrive_sem
):
    n = recv.shape[0]
    me, member = group_member()
    enter_group(n, me, member)
    scatter, update_total = scatter_sum(update_ref, recv, send_sem, recv_sem, me, member)
    out_ref[me] = (
        n * outer_ref[me]
        - (1.0 - inner_rate * decay_rate) * weight_ref[...]
        + inner_rate * update_total
    )
    gather = []
    for step in range(1, n):
        peer = (me + step) % n
        copy = pltpu.make_async_remote_copy(
            src_ref=out_ref.at[me],
            dst_ref=out_ref.at[me],
            send_sem=back_sem.at[peer],
            recv_sem=arrive_sem.at[me],
            device_id=member(peer),
            device_id_type=MESH,
        )
        copy.start()
        gather.append(copy)
    for step in range(1, n):
        sender = (me + n - step) % n
        pltpu.make_async_remote_copy(
            src_ref=out_ref.at[me],
            dst_ref=out_ref.at[sender],
            send_sem=back_sem.at[sender],
            recv_sem=arrive_sem.at[sender],
            device_id=member(sender),
            device_id_type=MESH,
        ).wait_recv()
    for copy in scatter + gather:
        copy.wait_send()


def group_blocks(values, dtype):
    n = 1
    for _, size in GROUP_PARTS:
        n *= size
    blocks = values.astype(dtype).reshape(n, -1, 128)
    rows = blocks.shape[1]
    padded = -(-rows // 16) * 16
    return jnp.pad(blocks, ((0, 0), (0, padded - rows), (0, 0))), rows


def weight_group_sum(weights):
    blocks, _ = group_blocks(weights, jnp.bfloat16)
    n = blocks.shape[0]
    return pl.pallas_call(
        weight_sum_kernel,
        out_shape=jax.ShapeDtypeStruct(blocks.shape[1:], jnp.float32),
        in_specs=[pl.BlockSpec(memory_space=pltpu.VMEM)],
        out_specs=pl.BlockSpec(memory_space=pltpu.VMEM),
        scratch_shapes=[pltpu.VMEM(blocks.shape, jnp.bfloat16)]
        + [pltpu.SemaphoreType.DMA((n,)) for _ in range(2)],
        compiler_params=pltpu.CompilerParams(collective_id=0, has_side_effects=True),
    )(blocks)


def pseudo_group_sum(update, weight_sum, outer):
    blocks, rows = group_blocks(update, jnp.bfloat16)
    outer_blocks, _ = group_blocks(outer, jnp.float32)
    n = blocks.shape[0]
    summed = pl.pallas_call(
        outer_sum_kernel,
        out_shape=jax.ShapeDtypeStruct(blocks.shape, jnp.float32),
        in_specs=[pl.BlockSpec(memory_space=pltpu.VMEM)] * 3,
        out_specs=pl.BlockSpec(memory_space=pltpu.VMEM),
        scratch_shapes=[pltpu.VMEM(blocks.shape, jnp.bfloat16)]
        + [pltpu.SemaphoreType.DMA((n,)) for _ in range(4)],
        compiler_params=pltpu.CompilerParams(collective_id=1, has_side_effects=True),
    )(blocks, weight_sum, outer_blocks)
    return summed[:, :rows].reshape(outer.shape)


def per_device(
    frames,
    cotangent,
    mix_partner,
    lengths,
    inner_params,
    first_moment,
    second_moment,
    outer_params,
    momentum,
):
    frame_rows = frames.shape[1]
    model_width = frames.shape[2]
    utt_count = mix_partner.shape[1]
    crop_frames = frame_rows // utt_count
    hidden_width = inner_params.shape[3]
    blocks = frames[0].reshape(utt_count, crop_frames, model_width).astype(jnp.float32)
    partner_rows = jnp.take(blocks, mix_partner[0], axis=0)
    mixed_rows = blocks + mix_weight * partner_rows
    normed = normalize(mixed_rows).reshape(frame_rows, model_width)
    offsets = lax.broadcasted_iota(jnp.int32, (utt_count, crop_frames), 1)
    keep_mask = (offsets < lengths[0][:, None]).reshape(frame_rows, 1).astype(jnp.bfloat16)
    masked_grad = cotangent[0] * keep_mask
    prologue = (gathered_order(normed), gathered_order(masked_grad))
    pieces, (normed, masked_grad), weight_sum = gather_pieces(inner_params[0], prologue)
    width = pieces[0].shape[0]
    normed_parts = [normed[:, i * width : (i + 1) * width] for i in range(len(pieces))]
    grad_parts = [masked_grad[:, i * width : (i + 1) * width] for i in range(len(pieces))]
    pre_sum = None
    back_sum = None
    for normed_part, grad_part, piece in zip(normed_parts, grad_parts, pieces):
        pre_term = jnp.dot(normed_part, piece[:, 0, :], preferred_element_type=jnp.float32)
        back_term = jnp.dot(grad_part, piece[:, 1, :], preferred_element_type=jnp.float32)
        pre_sum = pre_term if pre_sum is None else pre_sum + pre_term
        back_sum = back_term if back_sum is None else back_sum + back_term
    pre_act = pre_sum * model_width ** (-0.5)
    back_grad = back_sum * hidden_width ** (-0.5)
    activation, derivative = gelu_parts(pre_act)
    activation = activation.astype(jnp.bfloat16)
    hidden_grad = (back_grad * derivative).astype(jnp.bfloat16)

    grad_in = lax.dot_general(
        normed, hidden_grad, (((0,), (0,)), ((), ())), preferred_element_type=jnp.float32
    ) * model_width ** (-0.5)
    grad_out = lax.dot_general(
        masked_grad, activation, (((0,), (0,)), ((), ())), preferred_element_type=jnp.float32
    ) * hidden_width ** (-0.5)
    grads = jnp.stack((grad_in, grad_out), axis=1).astype(jnp.bfloat16)

    def piece_grad(index):
        return grads[index * width : (index + 1) * width]

    partner_rows = fold_core(piece_grad(1), piece_grad(3))
    partner_rows = lax.psum_scatter(partner_rows, "fx", scatter_dimension=0, tiled=True)
    own_rows = fold_core(piece_grad(0), piece_grad(2))
    own_rows, partner_rows = lax.optimization_barrier((own_rows, partner_rows))
    partner_rows = swap(partner_rows, "fz")
    own_rows = lax.psum_scatter(own_rows, "fx", scatter_dimension=0, tiled=True)
    gradients = own_rows.astype(jnp.float32) + partner_rows.astype(jnp.float32)
    new_moment = beta_one * first_moment[0] + (1.0 - beta_one) * gradients
    new_second = beta_two * second_moment[0] + (1.0 - beta_two) * gradients * gradients
    update = new_moment / correction_one / (jnp.sqrt(new_second / correction_two) + adam_eps)
    replica_count = 1
    for _, size in GROUP_PARTS:
        replica_count *= size
    totals = pseudo_group_sum(update, weight_sum, outer_params)
    average = totals * (1.0 / replica_count)
    new_momentum = nesterov_mu * momentum + average
    new_outer = outer_params - outer_rate * (average + nesterov_mu * new_momentum)
    return (new_moment[None], new_outer, new_momentum)


def solution(mesh):
    sizes = tuple(size for _, size in GROUP_PARTS + FSDP_PARTS)
    split_mesh = Mesh(mesh.devices.reshape(sizes), GROUP_AXES + FSDP_AXES)
    group, fsdp = GROUP_AXES, FSDP_AXES
    in_specs = (
        P(group, fsdp, None),
        P(group, fsdp, None),
        P(group, fsdp),
        P(group, fsdp),
        P(group, fsdp, None, None),
        P(group, fsdp, None, None),
        P(group, fsdp, None, None),
        P(fsdp, None, None),
        P(fsdp, None, None),
    )
    out_specs = (P(group, fsdp, None, None), P(fsdp, None, None), P(fsdp, None, None))
    return jax.shard_map(
        per_device, mesh=split_mesh, in_specs=in_specs, out_specs=out_specs, check_vma=False
    )
```
